32 devices in a mesh: pairs: 8 (over z, y), dom: 4 (over x, core).
Axes of the slice: x: 2, y: 2, z: 4, core: 2. Of those that a mesh axis runs over, the one named last changes fastest.
Arguments:
- amplitude: bfloat16 [64, 384, 384], P('pairs', 'dom'), may hold values from -2 to 2
- integrals: bfloat16 [64, 384, 384], P('pairs', 'dom'), may hold values from -6 to 6
- virtual_energy: float32 [64, 384], P('pairs'), may hold values from 0.2 to 1.5
- occupied_gap: float32 [64], P('pairs'), may hold values from 0.3 to 1.5
- pair_slot: int32 [64], replicated, may hold values from 0 to 63, as said below
- coupling_source: int32 [128], replicated, may hold values from 0 to 63, as said below
- coupling_target: int32 [128], replicated, may hold values from 0 to 63, as said below
- coupling_fock: float32 [128], P(('pairs', 'dom')), may hold values from -3 to 3
- coupling_intersection: bfloat16 [128, 384, 384], P(('pairs', 'dom')), may hold values from -0.3125 to 0.3125
Outputs:
- updated_amplitude: float32 [64, 384, 384], P('pairs', 'dom')
- residual: float32 [64, 384, 384], P('pairs', 'dom')
The draws below stay inside these ranges and needn't reach their ends.
Inputs may be any that keep to these rules, and one draw needn't show every extreme that they name: A permutation: pair p is stored at position pair_slot[p], which lies on index pair_slot[p] // 8 of pairs. `coupling_target`: coupling c is held by index c // 16 of pairs, and its target pair is stored on that same index; the two couplings that share a source pair on one holder have different targets. `coupling_source`: among the 16 couplings of one holder, every source pair appears in exactly two, and there are 8 distinct source pairs; of the pairs stored on any one index of pairs, a holder uses at most 2 distinct ones as sources, and exactly 2 for some indices on every holder.
All inputs are finite; a program needn't handle non-finite values.
Results may differ from the reference program's by a relative error of at most 0.0024.
Values may be sent and summed in bfloat16 or wider, within the bound.
A program may use at most 128 MiB of HBM per device.

```python
import math
import jax
import jax.numpy as jnp
from jax import lax

W = 384
PAIR_DEV = 8
UPDATES = 1
PAIRS = 64
CPL_DEV = 16
COUPLINGS = 128
N_DOM = 4


def shuffle_rows(keys, length):

    def one_row(row_key):
        return jax.random.permutation(row_key, length)
    return jax.vmap(one_row)(keys).astype(jnp.int32)


def coupling_tables(key):
    base = jax.random.fold_in(key, 7101)
    keys = jax.random.split(base, 8)
    holders = PAIRS // PAIR_DEV
    doubled = 3 * holders // 8
    single = holders // 4
    pair_slot = jax.random.permutation(keys[0], PAIRS).astype(jnp.int32)
    slot_pair = jnp.argsort(pair_slot).astype(jnp.int32)
    owner_order = shuffle_rows(jax.random.split(keys[1], holders), holders)
    twice = owner_order[:, :doubled]
    once = owner_order[:, doubled:doubled + single]
    first_local = jax.random.randint(keys[2], (holders, doubled), 0, PAIR_DEV)
    second_local = (first_local + 1 + jax.random.randint(keys[3], (holders, doubled), 0, PAIR_DEV - 1)) % PAIR_DEV
    once_local = jax.random.randint(keys[4], (holders, single), 0, PAIR_DEV)
    owners = jnp.concatenate([twice, twice, once], axis=1)
    local_index = jnp.concatenate([first_local, second_local, once_local], axis=1)
    sources = owners * PAIR_DEV + local_index
    first_target = jax.random.randint(keys[5], sources.shape, 0, PAIR_DEV)
    second_target = (first_target + 1 + jax.random.randint(keys[6], sources.shape, 0, PAIR_DEV - 1)) % PAIR_DEV
    holder_base = jnp.arange(holders, dtype=jnp.int32)[:, None] * PAIR_DEV
    source_all = jnp.concatenate([sources, sources], axis=1)
    target_all = jnp.concatenate([first_target, second_target], axis=1) + holder_base
    shuffle = shuffle_rows(jax.random.split(keys[7], holders), CPL_DEV)
    source_all = jnp.take_along_axis(source_all, shuffle, axis=1).reshape(-1)
    target_all = jnp.take_along_axis(target_all, shuffle, axis=1).reshape(-1)
    return (pair_slot, jnp.take(slot_pair, source_all).astype(jnp.int32), jnp.take(slot_pair, target_all).astype(jnp.int32))


def draw_pair_slot(key, part):
    return coupling_tables(key)[0]


def draw_coupling_source(key, part):
    return coupling_tables(key)[1]


def draw_coupling_target(key, part):
    return coupling_tables(key)[2]


def steps_of(key, shape, shards, low, high):
    level = 1.0
    for position, shards_of in shards:
        draws = jax.random.uniform(jax.random.fold_in(jax.random.fold_in(key, 6), position), (shards_of,), jnp.float32, low / len(shards), high / len(shards))
        level = level * jnp.repeat(jnp.exp(draws), shape[position] // shards_of).reshape((-1,) + (1,) * (len(shape) - 1 - position))
    return level


def gaussian(stream_key, dims, spread, most, shards=(), kind=jnp.bfloat16):
    entries = spread * jax.random.normal(stream_key, dims, jnp.float32)
    if shards:
        entries = entries * steps_of(stream_key, dims, shards, -0.22, 0.18)
    return jnp.clip(entries, -most, most).astype(kind)


def setup_inputs(seed: int = 0) -> dict:
    key_of = jax.random.split(jax.random.key(seed), 10)
    return {
        "amplitude": gaussian(key_of[0], (PAIRS, W, W), 0.3, 2.0, ((0, 8), (1, 4))),
        "integrals": gaussian(key_of[1], (PAIRS, W, W), 1.0, 6.0, ((0, 8), (1, 4))),
        "virtual_energy": jnp.clip(jnp.exp(math.log(1.5) - 2.014903 * jax.random.uniform(key_of[2], (PAIRS, W), jnp.float32) ** steps_of(key_of[2], (PAIRS, W), ((0, 8),), -0.2, 0.2)), 0.2, 1.5),
        "occupied_gap": jnp.clip(jnp.exp(math.log(1.5) - 1.60943787 * jax.random.uniform(key_of[3], (PAIRS,), jnp.float32) ** steps_of(key_of[3], (PAIRS,), ((0, 8),), -0.2, 0.2)), 0.3, 1.5),
        "pair_slot": draw_pair_slot(jax.random.fold_in(key_of[9], 71), 0),
        "coupling_source": draw_coupling_source(jax.random.fold_in(key_of[9], 71), 0),
        "coupling_target": draw_coupling_target(jax.random.fold_in(key_of[9], 71), 0),
        "coupling_fock": gaussian(key_of[7], (COUPLINGS,), 0.5, 3.0, ((0, 32),), jnp.float32),
        "coupling_intersection": gaussian(key_of[8], (COUPLINGS, W, W), W ** -0.5, 0.3125, ((0, 32),)),
    }


def reference(amplitude, integrals, virtual_energy, occupied_gap, pair_slot, coupling_source, coupling_target, coupling_fock, coupling_intersection):
    source_slot = jnp.take(pair_slot, coupling_source).astype(jnp.int32)
    target_slot = jnp.take(pair_slot, coupling_target).astype(jnp.int32)
    denominator = virtual_energy[:, :, None] + virtual_energy[:, None, :] + occupied_gap[:, None, None]
    current = amplitude.astype(jnp.float32)
    block = CPL_DEV // N_DOM
    blocks = COUPLINGS // block
    residual = jnp.zeros(current.shape, jnp.float32)
    for step in range(UPDATES):
        sent = current.astype(jnp.bfloat16)

        def add_block(total, index):
            start = (index * block).astype(jnp.int32)
            sources = lax.dynamic_slice_in_dim(source_slot, start, block)
            targets = lax.dynamic_slice_in_dim(target_slot, start, block)
            fock = lax.dynamic_slice_in_dim(coupling_fock, start, block)
            intersection = lax.dynamic_slice_in_dim(coupling_intersection, start, block).astype(jnp.float32)
            picked = jnp.take(sent, sources, axis=0).astype(jnp.float32)
            left = jnp.einsum("cab,cbd->cad", intersection, picked).astype(jnp.bfloat16)
            left = lax.optimization_barrier(left).astype(jnp.float32)
            projected = jnp.einsum("cad,ced->cae", left, intersection)
            coupled_term = (fock[:, None, None] * projected).astype(jnp.bfloat16)
            coupled_term = lax.optimization_barrier(coupled_term).astype(jnp.float32)
            return total.at[targets].add(coupled_term), None

        coupled, unused = lax.scan(add_block, jnp.zeros(current.shape, jnp.float32), jnp.arange(blocks, dtype=jnp.int32))
        residual = integrals.astype(jnp.float32) + denominator * current - coupled
        current = current - residual / denominator
    return current, residual
```

```python
import functools

import jax
import jax.numpy as jnp
from jax import lax
from jax.experimental import pallas as pl
from jax.experimental.pallas import tpu as pltpu
from jax.sharding import PartitionSpec as P

SRC_CAP = 2
CHUNK_ROWS = 16
VMEM_ROOM = 48 << 20
MESH = pl.DeviceIdType.MESH
VMEM = pltpu.VMEM
SMEM = pltpu.SMEM


def exchange_kernel(
    holders,
    quarters,
    slot_ref,
    source_ref,
    target_ref,
    fock_ref,
    amp_hbm,
    inter_hbm,
    terms_ref,
    local_ref,
    out_ref,
    inter_ref,
    held_ref,
    inter_sem,
    amp_ref,
    amp_sem,
    whole,
    picked,
    sent_terms,
    send1,
    recv1,
    local1,
    send2,
    recv2,
    send3,
    recv3,
    local3,
    inter_x,
    fock_out,
    fock_in,
    half_terms,
    swap_send,
    swap_recv,
    half_send,
    half_recv,
    half_local,
    *arrived,
):
    amp_copy = pltpu.make_async_copy(amp_hbm, amp_ref, amp_sem)
    amp_copy.start()
    me = lax.axis_index("pairs")
    quarter = lax.axis_index("dom")
    chunks = len(arrived)
    slots, chunk_rows, width = arrived[0].shape
    rows = chunk_rows * chunks
    group = inter_hbm.shape[0]
    half = holders // 2
    my_half = me // half
    in_half = me % half

    extra = whole.shape[0] - group
    full = group - extra
    partner = (quarter + quarters // 2) % quarters
    sibling = quarter + 1 - 2 * (quarter % 2)

    barrier = pltpu.get_barrier_semaphore()

    def greet(j, carry):
        pl.semaphore_signal(
            barrier, inc=1, device_id=((me + j) % holders, quarter), device_id_type=MESH
        )
        return carry

    lax.fori_loop(1, holders, greet, 0)
    for d in range(1, quarters):
        pl.semaphore_signal(
            barrier, inc=1, device_id=(me, (quarter + d) % quarters), device_id_type=MESH
        )

    def inter_copy(c):
        return pltpu.make_async_copy(inter_hbm.at[c], inter_ref.at[c], inter_sem.at[c])

    def fetch(c, carry):
        inter_copy(c).start()
        return carry

    lax.fori_loop(0, group, fetch, 0)

    pair_count = amp_ref.shape[0]
    couplings = source_ref.shape[0] // holders
    base = me * pair_count
    unroll = 8 if couplings % 8 == 0 else 1

    def holder_step(h, carry):
        def block(i, ab):
            first, second = ab
            for u in range(unroll):
                local = slot_ref[source_ref[h * couplings + i * unroll + u]] - base
                mine = (local >= 0) & (local < pair_count)
                free = first < 0
                second = jnp.where(mine & jnp.logical_not(free) & (local != first), local, second)
                first = jnp.where(mine & free, local, first)
            return first, second

        first, second = lax.fori_loop(
            0, couplings // unroll, block, (jnp.int32(-1), jnp.int32(-1))
        )
        out_ref[h * SRC_CAP] = amp_ref[jnp.maximum(first, 0)]
        out_ref[h * SRC_CAP + 1] = amp_ref[jnp.maximum(second, 0)]
        return carry

    fock_out[...] = jnp.full(fock_out.shape, fock_ref[group - 1], jnp.float32)
    amp_copy.wait()
    lax.fori_loop(0, holders, holder_step, 0)
    pl.semaphore_wait(barrier, holders - 1 + quarters - 1)

    def swaps():
        for i, (src, dst) in enumerate(((inter_hbm.at[group - 1], inter_x), (fock_out, fock_in))):
            yield pltpu.make_async_remote_copy(
                src_ref=src,
                dst_ref=dst,
                send_sem=swap_send.at[i],
                recv_sem=swap_recv.at[i],
                device_id=(me, partner),
                device_id_type=MESH,
            )

    if extra:
        for copy in swaps():
            copy.start()

    def owner_copy(k, h):
        span = pl.ds(k * chunk_rows, chunk_rows)
        return pltpu.make_async_remote_copy(
            src_ref=out_ref.at[pl.ds(h * SRC_CAP, SRC_CAP), span],
            dst_ref=arrived[k].at[pl.ds(me * SRC_CAP, SRC_CAP)],
            send_sem=send1.at[k, h],
            recv_sem=recv1.at[k, me],
            device_id=(h, quarter),
            device_id_type=MESH,
        )

    def arrival(k, h):
        span = pl.ds(k * chunk_rows, chunk_rows)
        return pltpu.make_async_remote_copy(
            src_ref=out_ref.at[pl.ds(h * SRC_CAP, SRC_CAP), span],
            dst_ref=arrived[k].at[pl.ds(h * SRC_CAP, SRC_CAP)],
            send_sem=send1.at[k, h],
            recv_sem=recv1.at[k, h],
            device_id=(h, quarter),
            device_id_type=MESH,
        )

    def own_copy(k):
        span = pl.ds(k * chunk_rows, chunk_rows)
        return pltpu.make_async_copy(
            out_ref.at[pl.ds(me * SRC_CAP, SRC_CAP), span],
            arrived[k].at[pl.ds(me * SRC_CAP, SRC_CAP)],
            local1.at[k],
        )

    for k in range(chunks):

        def far(j, carry, k=k):
            owner_copy(k, (1 - my_half) * half + (in_half + j) % half).start()
            return carry

        def near(j, carry, k=k):
            owner_copy(k, my_half * half + (in_half + j) % half).start()
            return carry

        lax.fori_loop(0, half, far, 0)
        lax.fori_loop(1, half, near, 0)
        own_copy(k).start()

    def own_step(c, carry):
        slot = slot_ref[source_ref[me * couplings + c]]
        owner = lax.div(slot, jnp.int32(pair_count))

        def block(i, first):
            for u in range(unroll):
                at = couplings - 1 - (i * unroll + u)
                other = slot_ref[source_ref[me * couplings + at]]
                same = lax.div(other, jnp.int32(pair_count)) == owner
                first = jnp.where(same, other, first)
            return first

        first = lax.fori_loop(0, couplings // unroll, block, slot)
        held_ref[c] = owner * SRC_CAP + jnp.where(first == slot, 0, 1)
        local_ref[c] = slot_ref[target_ref[me * couplings + c]] - base
        return carry

    lax.fori_loop(0, couplings, own_step, 0)

    def peer_copy(k, d):
        peer = (quarter + d) % quarters
        return pltpu.make_async_remote_copy(
            src_ref=picked.at[d - 1, k],
            dst_ref=whole.at[:, pl.ds(pl.multiple_of(quarter * rows + k * chunk_rows, 16), chunk_rows)],
            send_sem=send2.at[k, d],
            recv_sem=recv2.at[k, d],
            device_id=(me, peer),
            device_id_type=MESH,
        )

    def peer_arrival(k, d):
        peer = (quarter + quarters - d) % quarters
        return pltpu.make_async_remote_copy(
            src_ref=picked.at[d - 1, k],
            dst_ref=whole.at[:, pl.ds(pl.multiple_of(peer * rows + k * chunk_rows, 16), chunk_rows)],
            send_sem=send2.at[k, d],
            recv_sem=recv2.at[k, d],
            device_id=(me, peer),
            device_id_type=MESH,
        )

    for k in range(chunks):

        def take(j, carry, k=k):
            arrival(k, (me + j) % holders).wait_recv()
            return carry

        lax.fori_loop(1, holders, take, 0)
        own_copy(k).wait()
        picked_all = []
        for d in sorted(range(1, quarters), key=lambda d: abs(2 * d - quarters)):
            peer = (quarter + d) % quarters

            def pick(c, carry, k=k, d=d, peer=peer):
                picked[d - 1, k, c] = arrived[k][held_ref[peer * group + c]]
                return carry

            lax.fori_loop(0, group, pick, 0)
            if extra:
                last = ((peer + quarters // 2) % quarters) * group + group - 1
                picked[d - 1, k, group] = arrived[k][held_ref[last]]
            picked_all.append(d)
            if len(picked_all) == quarters - 1:
                for e in picked_all:
                    peer_copy(k, e).start()

        def keep(c, carry, k=k):
            start = pl.multiple_of(quarter * rows + k * chunk_rows, 16)
            whole[c, pl.ds(start, chunk_rows)] = arrived[k][held_ref[quarter * group + c]]
            return carry

        lax.fori_loop(0, group, keep, 0)
        if extra:
            start = pl.multiple_of(quarter * rows + k * chunk_rows, 16)
            last = partner * group + group - 1
            whole[group, pl.ds(start, chunk_rows)] = arrived[k][held_ref[last]]

    for k in range(chunks):
        for d in range(1, quarters):
            peer_arrival(k, d).wait_recv()

    def term_copy(c, d):
        peer = (quarter + d) % quarters
        return pltpu.make_async_remote_copy(
            src_ref=sent_terms.at[c, pl.ds(pl.multiple_of(peer * rows, 16), rows)],
            dst_ref=terms_ref.at[quarter * group + c],
            send_sem=send3.at[c, d],
            recv_sem=recv3.at[c, d],
            device_id=(me, peer),
            device_id_type=MESH,
        )

    def term_arrival(c, d):
        peer = (quarter + quarters - d) % quarters
        return pltpu.make_async_remote_copy(
            src_ref=sent_terms.at[c, pl.ds(pl.multiple_of(peer * rows, 16), rows)],
            dst_ref=terms_ref.at[peer * group + c],
            send_sem=send3.at[c, d],
            recv_sem=recv3.at[c, d],
            device_id=(me, peer),
            device_id_type=MESH,
        )

    def own_term(c):
        return pltpu.make_async_copy(
            sent_terms.at[c, pl.ds(pl.multiple_of(quarter * rows, 16), rows)],
            terms_ref.at[quarter * group + c],
            local3.at[c],
        )

    def multiply(c, carry):
        inter_copy(c).wait()
        inter = inter_ref[c]
        left = jnp.dot(inter, whole[c], preferred_element_type=jnp.float32).astype(jnp.bfloat16)
        projected = lax.dot_general(
            left, inter, (((1,), (1,)), ((), ())), preferred_element_type=jnp.float32
        )
        sent_terms[c] = (fock_ref[c] * projected).astype(jnp.bfloat16)
        for d in range(1, quarters):
            term_copy(c, d).start()
        own_term(c).start()
        return carry

    lax.fori_loop(0, full, multiply, 0)

    def half_copy(i):
        return pltpu.make_async_remote_copy(
            src_ref=half_terms.at[i, pl.ds(pl.multiple_of((sibling % 2) * rows, 16), rows)],
            dst_ref=terms_ref.at[(quarter, partner)[i] * group + group - 1],
            send_sem=half_send.at[i],
            recv_sem=half_recv.at[i],
            device_id=(me, sibling),
            device_id_type=MESH,
        )

    def half_arrival(i):
        owner = (sibling, (sibling + quarters // 2) % quarters)[i]
        return pltpu.make_async_remote_copy(
            src_ref=half_terms.at[i, pl.ds(pl.multiple_of((sibling % 2) * rows, 16), rows)],
            dst_ref=terms_ref.at[owner * group + group - 1],
            send_sem=half_send.at[i],
            recv_sem=half_recv.at[i],
            device_id=(me, sibling),
            device_id_type=MESH,
        )

    def half_own(i):
        return pltpu.make_async_copy(
            half_terms.at[i, pl.ds(pl.multiple_of((quarter % 2) * rows, 16), rows)],
            terms_ref.at[(quarter, partner)[i] * group + group - 1],
            half_local.at[i],
        )

    if extra:
        inter_copy(group - 1).wait()
        for copy in swaps():
            copy.wait_recv()
        own_half = pl.ds(pl.multiple_of((quarter // 2) * 2 * rows, 16), 2 * rows)
        for i in range(2):
            inter_i = inter_x if i else inter_ref.at[group - 1]
            scale = (fock_in if i else fock_out)[0:1, :]
            left = jnp.dot(
                inter_i[own_half, :], whole[group - 1 + i], preferred_element_type=jnp.float32
            ).astype(jnp.bfloat16)
            projected = lax.dot_general(
                left, inter_i[...], (((1,), (1,)), ((), ())), preferred_element_type=jnp.float32
            )
            half_terms[i] = (scale * projected).astype(jnp.bfloat16)
            half_copy(i).start()
            half_own(i).start()

    def finish(c, carry):
        for d in range(1, quarters):
            term_arrival(c, d).wait_recv()
        for d in range(1, quarters):
            term_copy(c, d).wait_send()
        own_term(c).wait()
        return carry

    lax.fori_loop(0, full, finish, 0)
    if extra:
        for i in range(2):
            half_arrival(i).wait_recv()
            half_copy(i).wait_send()
            half_own(i).wait()
        for copy in swaps():
            copy.wait_send()
    for k in range(chunks):

        def sent(j, carry, k=k):
            owner_copy(k, (me + j) % holders).wait_send()
            return carry

        lax.fori_loop(1, holders, sent, 0)
        for d in range(1, quarters):
            peer_copy(k, d).wait_send()


def spread_kernel(
    holders,
    split,
    slot_ref,
    source_ref,
    target_ref,
    fock_ref,
    amp_hbm,
    inter_hbm,
    terms_ref,
    local_ref,
    out_ref,
    amp_ref,
    amp_sem,
    inter_ref,
    inter_sem,
    held_ref,
    lead_ref,
    rank_ref,
    list_ref,
    pair_rows,
    full_terms,
    half_terms,
    fock_out,
    fock_in,
    send1,
    recv1,
    local1,
    send2,
    recv2,
    swap_send,
    swap_recv,
    send3,
    recv3,
    local3,
    half_send,
    half_recv,
    half_local,
    *arrived,
):
    amp_copy = pltpu.make_async_copy(amp_hbm, amp_ref, amp_sem)
    amp_copy.start()
    me = lax.axis_index("pairs")
    quarter = lax.axis_index("dom")
    chunks = len(arrived)
    slots, chunk_rows, width = arrived[0].shape
    rows = chunk_rows * chunks
    group = inter_hbm.shape[0]
    distinct = pair_rows.shape[0]
    half = holders // 2
    my_half = me // half
    in_half = me % half
    sibling = quarter + 1 - 2 * (quarter % 2)
    across = (quarter + 2) % 4
    diagonal = sibling + 2 - 4 * (sibling // 2)
    chip_start = pl.multiple_of((quarter // 2) * 2 * rows, 16)

    barrier = pltpu.get_barrier_semaphore()

    def greet(j, carry):
        pl.semaphore_signal(
            barrier, inc=1, device_id=((me + j) % holders, quarter), device_id_type=MESH
        )
        return carry

    lax.fori_loop(1, holders, greet, 0)
    for peer in (sibling, across, diagonal):
        pl.semaphore_signal(barrier, inc=1, device_id=(me, peer), device_id_type=MESH)

    def inter_copy(c):
        return pltpu.make_async_copy(inter_hbm.at[c], inter_ref.at[c], inter_sem.at[c])

    for c in range(group):
        inter_copy(c).start()
    for c in range(split):
        fock_out[c] = jnp.full(fock_out.shape[1:], fock_ref[c], jnp.float32)

    pair_count = amp_ref.shape[0]
    couplings = source_ref.shape[0] // holders
    base = me * pair_count
    unroll = 8 if couplings % 8 == 0 else 1

    def choose(h):
        def block(i, ab):
            first, second = ab
            for u in range(unroll):
                local = slot_ref[source_ref[h * couplings + i * unroll + u]] - base
                mine = (local >= 0) & (local < pair_count)
                free = first < 0
                second = jnp.where(mine & jnp.logical_not(free) & (local != first), local, second)
                first = jnp.where(mine & free, local, first)
            return first, second

        first, second = lax.fori_loop(
            0, couplings // unroll, block, (jnp.int32(-1), jnp.int32(-1))
        )
        out_ref[h * SRC_CAP] = amp_ref[jnp.maximum(first, 0)]
        out_ref[h * SRC_CAP + 1] = amp_ref[jnp.maximum(second, 0)]

    def far_holder(j):
        return (1 - my_half) * half + (in_half + j) % half

    def near_holder(j):
        return my_half * half + (in_half + j) % half

    def choose_far(j, carry):
        choose(far_holder(j))
        return carry

    def choose_near(j, carry):
        choose(near_holder(j))
        return carry

    amp_copy.wait()
    lax.fori_loop(0, half, choose_far, 0)
    pl.semaphore_wait(barrier, holders - 1 + 3)

    def owner_copy(k, h):
        span = pl.ds(k * chunk_rows, chunk_rows)
        return pltpu.make_async_remote_copy(
            src_ref=out_ref.at[pl.ds(h * SRC_CAP, SRC_CAP), span],
            dst_ref=arrived[k].at[pl.ds(me * SRC_CAP, SRC_CAP)],
            send_sem=send1.at[k, h],
            recv_sem=recv1.at[k, me],
            device_id=(h, quarter),
            device_id_type=MESH,
        )

    def arrival(k, h):
        span = pl.ds(k * chunk_rows, chunk_rows)
        return pltpu.make_async_remote_copy(
            src_ref=out_ref.at[pl.ds(h * SRC_CAP, SRC_CAP), span],
            dst_ref=arrived[k].at[pl.ds(h * SRC_CAP, SRC_CAP)],
            send_sem=send1.at[k, h],
            recv_sem=recv1.at[k, h],
            device_id=(h, quarter),
            device_id_type=MESH,
        )

    def own_copy(k):
        span = pl.ds(k * chunk_rows, chunk_rows)
        return pltpu.make_async_copy(
            out_ref.at[pl.ds(me * SRC_CAP, SRC_CAP), span],
            arrived[k].at[pl.ds(me * SRC_CAP, SRC_CAP)],
            local1.at[k],
        )

    def send_far(k):
        def far(j, carry):
            owner_copy(k, far_holder(j)).start()
            return carry

        lax.fori_loop(0, half, far, 0)

    def send_near(k):
        def near(j, carry):
            owner_copy(k, near_holder(j)).start()
            return carry

        lax.fori_loop(1, half, near, 0)
        own_copy(k).start()

    def swaps():
        for c in range(split):
            yield pltpu.make_async_remote_copy(
                src_ref=inter_hbm.at[c],
                dst_ref=inter_ref.at[group + c],
                send_sem=swap_send.at[c],
                recv_sem=swap_recv.at[c],
                device_id=(me, across),
                device_id_type=MESH,
            )
        yield pltpu.make_async_remote_copy(
            src_ref=fock_out,
            dst_ref=fock_in,
            send_sem=swap_send.at[split],
            recv_sem=swap_recv.at[split],
            device_id=(me, across),
            device_id_type=MESH,
        )

    send_far(0)
    for copy in swaps():
        copy.start()
    lax.fori_loop(0, half, choose_near, 0)
    send_near(0)
    for k in range(1, chunks):
        send_far(k)
        send_near(k)

    def own_step(c, count):
        pair = source_ref[me * couplings + c]
        slot = slot_ref[pair]
        owner = lax.div(slot, jnp.int32(pair_count))

        def block(i, carry):
            first, lead = carry
            for u in range(unroll):
                at = couplings - 1 - (i * unroll + u)
                other_pair = source_ref[me * couplings + at]
                other = slot_ref[other_pair]
                same = lax.div(other, jnp.int32(pair_count)) == owner
                first = jnp.where(same, other, first)
                lead = jnp.where(other_pair == pair, at, lead)
            return first, lead

        first, lead = lax.fori_loop(0, couplings // unroll, block, (slot, c))
        held_ref[c] = owner * SRC_CAP + jnp.where(first == slot, 0, 1)
        lead_ref[c] = lead
        rank_ref[c] = count
        local_ref[c] = slot_ref[target_ref[me * couplings + c]] - base
        return count + jnp.where(lead == c, 1, 0)

    lax.fori_loop(0, couplings, own_step, jnp.int32(0))

    def list_step(j, carry):
        def block(i, found):
            for u in range(unroll):
                c = i * unroll + u
                found = jnp.where((lead_ref[c] == c) & (rank_ref[c] == j), held_ref[c], found)
            return found

        list_ref[j] = lax.fori_loop(0, couplings // unroll, block, jnp.int32(0))
        return carry

    lax.fori_loop(0, distinct, list_step, 0)

    def span_of(owner, k):
        start = pl.multiple_of(owner * rows + k * chunk_rows, 16)
        return pair_rows.at[:, pl.ds(start, chunk_rows)]

    def rows_copy(kind, k, owner, peer, landed):
        return pltpu.make_async_remote_copy(
            src_ref=span_of(owner, k),
            dst_ref=span_of(landed, k),
            send_sem=send2.at[kind, k],
            recv_sem=recv2.at[kind, k],
            device_id=(me, peer),
            device_id_type=MESH,
        )

    def across_copy(k):
        return rows_copy(0, k, quarter, across, quarter)

    def across_arrival(k):
        return rows_copy(0, k, quarter, across, across)

    def sibling_copy(k):
        return rows_copy(1, k, quarter, sibling, quarter)

    def sibling_arrival(k):
        return rows_copy(1, k, quarter, sibling, sibling)

    def relay_copy(k):
        return rows_copy(2, k, across, sibling, across)

    def relay_arrival(k):
        return rows_copy(2, k, across, sibling, diagonal)

    def take_chunk(k):
        def take(j, carry):
            arrival(k, (me + j) % holders).wait_recv()
            return carry

        lax.fori_loop(1, holders, take, 0)
        own_copy(k).wait()
        start = pl.multiple_of(quarter * rows + k * chunk_rows, 16)

        def pick(j, carry):
            pair_rows[j, pl.ds(start, chunk_rows)] = arrived[k][list_ref[j]]
            return carry

        lax.fori_loop(0, distinct, pick, 0)
        across_copy(k).start()
        sibling_copy(k).start()

    def relay_chunk(k):
        across_arrival(k).wait_recv()
        relay_copy(k).start()

    relayed = 0
    for k in range(chunks):
        take_chunk(k)
        if k >= 2:
            relay_chunk(relayed)
            relayed += 1
    while relayed < chunks:
        relay_chunk(relayed)
        relayed += 1
    for k in range(chunks):
        sibling_arrival(k).wait_recv()
        relay_arrival(k).wait_recv()

    def source_of(owner, c):
        return rank_ref[lead_ref[owner * group + c]]

    def full_copy(c, peer, at):
        return pltpu.make_async_remote_copy(
            src_ref=full_terms.at[c, pl.ds(pl.multiple_of(peer * rows, 16), rows)],
            dst_ref=terms_ref.at[quarter * group + split + c],
            send_sem=send3.at[c, at],
            recv_sem=recv3.at[c, at],
            device_id=(me, peer),
            device_id_type=MESH,
        )

    def full_arrival(c, peer, at):
        return pltpu.make_async_remote_copy(
            src_ref=full_terms.at[c, pl.ds(pl.multiple_of(peer * rows, 16), rows)],
            dst_ref=terms_ref.at[peer * group + split + c],
            send_sem=send3.at[c, at],
            recv_sem=recv3.at[c, at],
            device_id=(me, peer),
            device_id_type=MESH,
        )

    def full_own(c):
        return pltpu.make_async_copy(
            full_terms.at[c, pl.ds(pl.multiple_of(quarter * rows, 16), rows)],
            terms_ref.at[quarter * group + split + c],
            local3.at[c],
        )

    peers = (across, diagonal, sibling)

    for c in range(group):
        inter_copy(c).wait()

    def multiply(c, carry):
        inter = inter_ref[split + c]
        left = jnp.dot(
            inter, pair_rows[source_of(quarter, split + c)], preferred_element_type=jnp.float32
        ).astype(jnp.bfloat16)
        projected = lax.dot_general(
            left, inter, (((1,), (1,)), ((), ())), preferred_element_type=jnp.float32
        )
        full_terms[c] = (fock_ref[split + c] * projected).astype(jnp.bfloat16)
        for at, peer in enumerate(peers):
            full_copy(c, peer, at).start()
        full_own(c).start()
        return carry

    lax.fori_loop(0, group - split, multiply, 0)

    def half_copy(i, owner, c):
        return pltpu.make_async_remote_copy(
            src_ref=half_terms.at[i, pl.ds(pl.multiple_of((sibling % 2) * rows, 16), rows)],
            dst_ref=terms_ref.at[owner * group + c],
            send_sem=half_send.at[i],
            recv_sem=half_recv.at[i],
            device_id=(me, sibling),
            device_id_type=MESH,
        )

    def half_own(i, owner, c):
        return pltpu.make_async_copy(
            half_terms.at[i, pl.ds(pl.multiple_of((quarter % 2) * rows, 16), rows)],
            terms_ref.at[owner * group + c],
            half_local.at[i],
        )

    own_rows = pl.ds(chip_start, 2 * rows)
    for copy in swaps():
        copy.wait_recv()
    for side in range(2):

        def multiply_half(c, carry, side=side):
            owner = across if side else quarter
            scale = fock_in[c, 0:1, :] if side else fock_ref[c]
            inter = inter_ref.at[side * group + c]
            left = jnp.dot(
                inter[own_rows, :],
                pair_rows[source_of(owner, c)],
                preferred_element_type=jnp.float32,
            ).astype(jnp.bfloat16)
            projected = lax.dot_general(
                left, inter[...], (((1,), (1,)), ((), ())), preferred_element_type=jnp.float32
            )
            half_terms[side * split + c] = (scale * projected).astype(jnp.bfloat16)
            half_copy(side * split + c, owner, c).start()
            half_own(side * split + c, owner, c).start()
            return carry

        lax.fori_loop(0, split, multiply_half, 0)

    def finish(c, carry):
        for at, peer in enumerate(peers):
            full_arrival(c, peer, at).wait_recv()
        for at, peer in enumerate(peers):
            full_copy(c, peer, at).wait_send()
        full_own(c).wait()
        return carry

    lax.fori_loop(0, group - split, finish, 0)
    for side in range(2):

        def finish_half(c, carry, side=side):
            i = side * split + c
            half_copy(i, diagonal if side else sibling, c).wait_recv()
            half_copy(i, across if side else quarter, c).wait_send()
            half_own(i, across if side else quarter, c).wait()
            return carry

        lax.fori_loop(0, split, finish_half, 0)
    for copy in swaps():
        copy.wait_send()
    for k in range(chunks):

        def sent(j, carry, k=k):
            owner_copy(k, (me + j) % holders).wait_send()
            return carry

        lax.fori_loop(1, holders, sent, 0)
        across_copy(k).wait_send()
        sibling_copy(k).wait_send()
        relay_copy(k).wait_send()


def update_kernel(
    local_ref,
    gap_ref,
    terms_hbm,
    amp_hbm,
    integrals_hbm,
    energy_ref,
    new_hbm,
    residual_hbm,
    terms,
    amp,
    integrals,
    new,
    residual,
    columns,
    term_sem,
    in_sem,
    out_sem,
):
    quarter = lax.axis_index("dom")
    couplings = terms.shape[0]
    pair_count, rows, width = amp.shape

    def term_copy(c):
        return pltpu.make_async_copy(terms_hbm.at[c], terms.at[c], term_sem.at[c])

    def in_copies(p):
        return (
            pltpu.make_async_copy(amp_hbm.at[p], amp.at[p], in_sem.at[0, p]),
            pltpu.make_async_copy(integrals_hbm.at[p], integrals.at[p], in_sem.at[1, p]),
        )

    def out_copies(p):
        return (
            pltpu.make_async_copy(new.at[p], new_hbm.at[p], out_sem.at[0, p]),
            pltpu.make_async_copy(residual.at[p], residual_hbm.at[p], out_sem.at[1, p]),
        )

    def start_term(c, carry):
        term_copy(c).start()
        return carry

    for p in range(pair_count):
        for copy in in_copies(p):
            copy.start()
    lax.fori_loop(0, couplings, start_term, 0)
    columns[...] = jnp.transpose(energy_ref[...])
    own_rows = columns[pl.ds(pl.multiple_of(quarter * rows, 8), rows), :]

    def denominator(p):
        return own_rows[:, p : p + 1] + energy_ref[p : p + 1, :] + gap_ref[p]

    for p in range(pair_count):
        for copy in in_copies(p):
            copy.wait()
        current = amp[p].astype(jnp.float32)
        residual[p] = integrals[p].astype(jnp.float32) + denominator(p) * current

    def add_term(c, carry):
        term_copy(c).wait()
        p = local_ref[c]
        residual[p] = residual[p] - terms[c].astype(jnp.float32)
        return carry

    lax.fori_loop(0, couplings, add_term, 0)
    for p in range(pair_count):
        new[p] = amp[p].astype(jnp.float32) - residual[p] / denominator(p)
        for copy in out_copies(p):
            copy.start()
    for p in range(pair_count):
        for copy in out_copies(p):
            copy.wait()


def per_device(
    amplitude,
    integrals,
    virtual_energy,
    occupied_gap,
    pair_slot,
    coupling_source,
    coupling_target,
    coupling_fock,
    coupling_intersection,
):
    holders = lax.axis_size("pairs")
    quarters = lax.axis_size("dom")
    own_quarter = lax.axis_index("dom")
    pair_count, rows, width = amplitude.shape
    couplings = coupling_source.shape[0] // holders
    group = coupling_intersection.shape[0]
    slots = holders * SRC_CAP
    extra = 1 if quarters == 4 and group > 1 else 0
    chunk_rows = CHUNK_ROWS if rows % CHUNK_ROWS == 0 else rows
    chunks = rows // chunk_rows
    bf16 = jnp.bfloat16
    in_vmem = pl.BlockSpec(memory_space=VMEM)
    in_smem = pl.BlockSpec(memory_space=SMEM)
    anywhere = pl.BlockSpec(memory_space=pl.ANY)

    dma = pltpu.SemaphoreType.DMA
    distinct = couplings // 2
    whole_rows = quarters * rows
    held_rows = (
        2 * slots
        + pair_count
        + quarters * (2 * group + distinct)
        + 2 * group
    ) * rows
    fits = 2 * width * held_rows <= VMEM_ROOM
    if quarters == 4 and group >= 2 and group % 2 == 0 and holders % 2 == 0 and fits:
        split = group // 2
        terms, local = pl.pallas_call(
            functools.partial(spread_kernel, holders, split),
            out_shape=(
                jax.ShapeDtypeStruct((couplings, rows, width), bf16),
                jax.ShapeDtypeStruct((couplings,), jnp.int32),
            ),
            in_specs=[in_smem, in_smem, in_smem, in_smem, anywhere, anywhere],
            out_specs=(anywhere, in_smem),
            scratch_shapes=[
                VMEM((slots, rows, width), bf16),
                VMEM((pair_count, rows, width), bf16),
                dma(()),
                VMEM((group + split, whole_rows, width), bf16),
                dma((group,)),
                SMEM((couplings,), jnp.int32),
                SMEM((couplings,), jnp.int32),
                SMEM((couplings,), jnp.int32),
                SMEM((distinct,), jnp.int32),
                VMEM((distinct, whole_rows, width), bf16),
                VMEM((group - split, whole_rows, width), bf16),
                VMEM((2 * split, 2 * rows, width), bf16),
                VMEM((split, 8, width), jnp.float32),
                VMEM((split, 8, width), jnp.float32),
                dma((chunks, holders)),
                dma((chunks, holders)),
                dma((chunks,)),
                dma((3, chunks)),
                dma((3, chunks)),
                dma((split + 1,)),
                dma((split + 1,)),
                dma((group - split, 3)),
                dma((group - split, 3)),
                dma((group - split,)),
                dma((2 * split,)),
                dma((2 * split,)),
                dma((2 * split,)),
            ]
            + [VMEM((slots, chunk_rows, width), bf16)] * chunks,
            compiler_params=pltpu.CompilerParams(
                collective_id=0, has_side_effects=True, vmem_limit_bytes=60 << 20
            ),
            name="exchange",
        )(pair_slot, coupling_source, coupling_target, coupling_fock, amplitude, coupling_intersection)
    else:
        terms, local = pl.pallas_call(
            functools.partial(exchange_kernel, holders, quarters),
            out_shape=(
                jax.ShapeDtypeStruct((couplings, rows, width), bf16),
                jax.ShapeDtypeStruct((couplings,), jnp.int32),
            ),
            in_specs=[in_smem, in_smem, in_smem, in_smem, anywhere, anywhere],
            out_specs=(anywhere, in_smem),
            scratch_shapes=[
                VMEM((slots, rows, width), bf16),
                VMEM((group, quarters * rows, width), bf16),
                SMEM((couplings,), jnp.int32),
                dma((group,)),
                VMEM((pair_count, rows, width), bf16),
                dma(()),
                VMEM((group + extra, quarters * rows, width), bf16),
                VMEM((quarters - 1, chunks, group + extra, chunk_rows, width), bf16),
                VMEM((group, quarters * rows, width), bf16),
                dma((chunks, holders)),
                dma((chunks, holders)),
                dma((chunks,)),
                dma((chunks, quarters)),
                dma((chunks, quarters)),
                dma((group, quarters)),
                dma((group, quarters)),
                dma((group,)),
                VMEM((quarters * rows, width), bf16),
                VMEM((8, width), jnp.float32),
                VMEM((8, width), jnp.float32),
                VMEM((2, 2 * rows, width), bf16),
                dma((2,)),
                dma((2,)),
                dma((2,)),
                dma((2,)),
                dma((2,)),
            ]
            + [VMEM((slots, chunk_rows, width), bf16)] * chunks,
            compiler_params=pltpu.CompilerParams(
                collective_id=0, has_side_effects=True, vmem_limit_bytes=60 << 20
            ),
            name="exchange",
        )(pair_slot, coupling_source, coupling_target, coupling_fock, amplitude, coupling_intersection)

    out = jax.ShapeDtypeStruct((pair_count, rows, width), jnp.float32)
    return pl.pallas_call(
        update_kernel,
        out_shape=(out, out),
        in_specs=[in_smem, in_smem, anywhere, anywhere, anywhere, in_vmem],
        out_specs=(anywhere, anywhere),
        scratch_shapes=[
            VMEM((couplings, rows, width), bf16),
            VMEM((pair_count, rows, width), bf16),
            VMEM((pair_count, rows, width), bf16),
            VMEM((pair_count, rows, width), jnp.float32),
            VMEM((pair_count, rows, width), jnp.float32),
            VMEM((width, pair_count), jnp.float32),
            dma((couplings,)),
            dma((2, pair_count)),
            dma((2, pair_count)),
        ],
        name="update",
    )(local, occupied_gap, terms, amplitude, integrals, virtual_energy)


def solution(mesh):
    in_specs = (
        P("pairs", "dom", None),
        P("pairs", "dom", None),
        P("pairs", None),
        P("pairs"),
        P(),
        P(),
        P(),
        P(("pairs", "dom")),
        P(("pairs", "dom"), None, None),
    )
    out_specs = (P("pairs", "dom", None), P("pairs", "dom", None))
    return jax.shard_map(
        per_device, mesh=mesh, in_specs=in_specs, out_specs=out_specs, check_vma=False
    )
```
